32 devices in a mesh: grp: 2 (over y), seq: 4 (over z), head: 4 (over x, core).
Axes of the slice: x: 2, y: 2, z: 4, core: 2. Of those that a mesh axis runs over, the one named last changes fastest.
Arguments:
- queries: bfloat16 [4096, 8192], P(('grp', 'seq'), 'head'), parts along dimension 0, may hold values from -1.796875 to 1.796875
- key_vectors: bfloat16 [4096, 8192], P(('grp', 'seq'), 'head'), parts along dimension 0, may hold values from -1.796875 to 1.796875
- values: bfloat16 [4096, 8192], P(('grp', 'seq'), 'head'), parts along dimension 0, may hold values from -6 to 6
- decay_log: float32 [64, 4096], P('head', ('grp', 'seq')), parts along dimension 1, may hold values from -1 to 0, as said below
- norm_gain: float32 [8192], P('head'), may hold values from 0.1 to 1.9
- out_grad: bfloat16 [4096, 8192], P(('grp', 'seq'), 'head'), parts along dimension 0, may hold values from -6 to 6
Outputs:
- normed_out: bfloat16 [4096, 8192], P(('grp', 'seq'), 'head'), parts along dimension 0
- grad_queries: bfloat16 [4096, 8192], P(('grp', 'seq'), 'head'), parts along dimension 0
- grad_keys: bfloat16 [4096, 8192], P(('grp', 'seq'), 'head'), parts along dimension 0
- grad_values: bfloat16 [4096, 8192], P(('grp', 'seq'), 'head'), parts along dimension 0
- gain_grad: float32 [16384], P(('grp', 'head')), parts along dimension 0
The draws below stay inside these ranges and needn't reach their ends.
There are 2 independent parts, one for each index of `grp`. The reference program is written for one: setup_inputs(seed, part) draws one part's arguments, and reference() takes and returns one part's arrays. A program takes and returns all parts, laid end to end along the dimension named above; an argument that names none is the same for every part. Nothing has to cross between parts.
Inputs may be any that keep to these rules, and one draw needn't show every extreme that they name: `decay_log`: never positive.
All inputs are finite; a program needn't handle non-finite values.
Results may differ from the reference program's by a relative error of at most 0.0085.
Values sent between devices are 32-bit elements; how exact they have to be, the bound alone decides.
A program may use at most 128 MiB of HBM per device.

```python
import jax
import jax.numpy as jnp
from jax import lax

HEAD_COUNT = 64
HEAD_DIM = 128
TOK_DEV = 512
TOKEN_COUNT = 2048
FEATURES = 8192
N_SEQ = 4


def draw_decay_log(key, part):
    key_blocks_split = jax.random.split(jax.random.fold_in(key, 17), 7)
    slow_heads = jax.random.uniform(key_blocks_split[0], (HEAD_COUNT, 1)) < 0.5
    slow_rate = jnp.exp(jax.random.uniform(key_blocks_split[1], (HEAD_COUNT, 1), minval=jnp.log(0.1), maxval=jnp.log(1.0))) / TOKEN_COUNT
    fast_rate = jnp.exp(jax.random.uniform(key_blocks_split[2], (HEAD_COUNT, 1), minval=jnp.log(0.02), maxval=jnp.log(0.04)))
    baseline_decay_rate = jnp.where(slow_heads, slow_rate, fast_rate)
    block_decay_factor = jnp.exp(jax.random.uniform(key_blocks_split[3], (HEAD_COUNT, TOKEN_COUNT // TOK_DEV, 1), minval=jnp.log(0.5), maxval=jnp.log(2.0)))
    block_decay_factor = jnp.broadcast_to(block_decay_factor, (HEAD_COUNT, TOKEN_COUNT // TOK_DEV, TOK_DEV)).reshape(HEAD_COUNT, TOKEN_COUNT)
    position_decay_factor = jax.random.uniform(key_blocks_split[4], (HEAD_COUNT, TOKEN_COUNT), minval=0.5, maxval=1.5)
    sequence_blocks = jax.random.uniform(key_blocks_split[5], (HEAD_COUNT, TOKEN_COUNT)) < 3.0 / TOKEN_COUNT
    block_length = jax.random.uniform(key_blocks_split[6], (HEAD_COUNT, TOKEN_COUNT), minval=0.22, maxval=0.69)
    final_output = -(baseline_decay_rate * block_decay_factor * position_decay_factor) - jnp.where(sequence_blocks, block_length, 0.0)
    return final_output.astype(jnp.float32)


def levels(stream_key, dims, shards, low, high):
    def one(dim, parts):
        heights = jax.random.uniform(jax.random.fold_in(jax.random.fold_in(stream_key, 6), dim), (parts,), jnp.float32, low / len(shards), high / len(shards))
        return jnp.repeat(jnp.exp(heights), dims[dim] // parts).reshape((-1,) + (1,) * (len(dims) - dim - 1))

    gain = one(*shards[0])
    for cut in shards[1:]:
        gain = gain * one(*cut)
    return gain


def scatter_about(key, dims, scale, reach, cuts=(), kind=jnp.bfloat16):
    gain = levels(key, dims, cuts, -0.22, 0.18) if cuts else 1.0
    values = jax.random.normal(key, dims, jnp.float32) * scale * gain
    return jnp.minimum(jnp.maximum(values, -reach), reach).astype(kind)


def setup_inputs(seed: int = 0, part: int = 0) -> dict:
    seeds = jax.random.split(jax.random.key(seed), 7)
    own_keys = jax.random.split(jax.random.fold_in(seeds[6], part), 7)
    queries = scatter_about(own_keys[0], (TOKEN_COUNT, FEATURES), 0.3, 1.796875, ((0, 4), (1, 4)))
    key_vectors = scatter_about(own_keys[1], (TOKEN_COUNT, FEATURES), 0.3, 1.796875, ((0, 4), (1, 4)))
    values = scatter_about(own_keys[2], (TOKEN_COUNT, FEATURES), 1.0, 6.0, ((0, 4), (1, 4)))
    decay_log = draw_decay_log(jax.random.fold_in(jax.random.fold_in(seeds[6], part), 71), part)
    norm_gain = jnp.clip(1.0 + 0.18 * jax.random.normal(seeds[4], (FEATURES,), jnp.float32), 0.1, 1.9)
    out_grad = scatter_about(own_keys[5], (TOKEN_COUNT, FEATURES), 1.0, 6.0, ((0, 4), (1, 4)))
    return dict(queries=queries, key_vectors=key_vectors, values=values, decay_log=decay_log, norm_gain=norm_gain, out_grad=out_grad)


eps_norm = 1e-06
maximum_precision = lax.Precision.HIGHEST

def rounded(array):
    return lax.optimization_barrier(array.astype(jnp.bfloat16)).astype(jnp.float32)

def block_weight(cumulative):
    row_count = cumulative.shape[1]
    spread = cumulative[:, :, None] - cumulative[:, None, :]
    causal = jnp.arange(row_count)[:, None] >= jnp.arange(row_count)[None, :]
    return jnp.where(causal[None], jnp.exp(jnp.minimum(spread, 0.0)), 0.0)

def reference(queries, key_vectors, values, decay_log, norm_gain, out_grad):

    def split_heads(array):
        return array.astype(jnp.float32).reshape(N_SEQ, TOK_DEV, HEAD_COUNT, HEAD_DIM)
    query_all = split_heads(queries)
    key_all = split_heads(key_vectors)
    value_all = split_heads(values)
    cumulative = jnp.cumsum(decay_log.reshape(HEAD_COUNT, N_SEQ, TOK_DEV).transpose(1, 0, 2), axis=2)

    def forward(incoming_state, block_data):
        query_heads, key_heads, value_per_head, cumul_block = block_data
        totals = cumul_block[:, -1]
        weight = block_weight(cumul_block)
        rising = jnp.exp(cumul_block).T[:, :, None]
        falling = jnp.exp(totals[:, None] - cumul_block).T[:, :, None]
        query_growing_decay = rounded(query_heads * rising)
        key_shrinking_decay = rounded(key_heads * falling)
        state_reduced = rounded(incoming_state)
        scores = rounded(jnp.einsum('thd,shd->hts', query_heads, key_heads, precision=maximum_precision) * weight)
        attention_output = jnp.einsum('hts,shv->thv', scores, value_per_head, precision=maximum_precision)
        attention_output = attention_output + jnp.einsum('ilf,lfg->ilg', query_growing_decay, state_reduced, precision=maximum_precision)
        block_local_state = jnp.einsum('isx,isl->sxl', key_shrinking_decay, value_per_head, precision=maximum_precision)
        state_out = jnp.exp(totals)[:, None, None] * incoming_state + block_local_state
        return (state_out, (rounded(attention_output), state_reduced))
    zero_state = jnp.zeros((HEAD_COUNT, HEAD_DIM, HEAD_DIM), jnp.float32)
    _, (attended_all, states_low) = lax.scan(forward, zero_state, (query_all, key_all, value_all, cumulative))
    attention_output = attended_all.reshape(TOKEN_COUNT, FEATURES)
    inv_rms = lax.rsqrt(lax.optimization_barrier(jnp.mean(attention_output * attention_output, axis=1)) + eps_norm)
    normed = attention_output * inv_rms[:, None]
    normed_out = (normed * norm_gain).astype(jnp.bfloat16)
    grad_out = out_grad.astype(jnp.float32)
    gain_grad = lax.optimization_barrier(jnp.sum(grad_out * normed, axis=0))
    grad_normed = grad_out * norm_gain
    projection = lax.optimization_barrier(jnp.mean(grad_normed * normed, axis=1))
    grad_att = rounded(inv_rms[:, None] * (grad_normed - normed * projection[:, None]))
    grad_att_all = grad_att.reshape(N_SEQ, TOK_DEV, HEAD_COUNT, HEAD_DIM)

    def backward(back_state, block_data):
        query_heads, key_heads, value_per_head, cumul_block, gradient_per_head, state_reduced = block_data
        totals = cumul_block[:, -1]
        weight = block_weight(cumul_block)
        rising = jnp.exp(cumul_block).T[:, :, None]
        falling = jnp.exp(totals[:, None] - cumul_block).T[:, :, None]
        query_growing_decay = rounded(query_heads * rising)
        key_shrinking_decay = rounded(key_heads * falling)
        value_shrinking_decay = rounded(value_per_head * falling)
        gradient_growing_decay = rounded(gradient_per_head * rising)
        backward_state_reduced = rounded(back_state)
        scores = rounded(jnp.einsum('thd,shd->hts', query_heads, key_heads, precision=maximum_precision) * weight)
        grad_scores = rounded(jnp.einsum('thd,shd->hts', gradient_per_head, value_per_head, precision=maximum_precision) * weight)
        query_gradient = jnp.einsum('hts,shd->thd', grad_scores, key_heads, precision=maximum_precision)
        query_gradient = query_gradient + jnp.einsum('rad,afd->raf', gradient_growing_decay, state_reduced, precision=maximum_precision)
        key_gradient = jnp.einsum('hts,thd->shd', grad_scores, query_heads, precision=maximum_precision)
        key_gradient = key_gradient + jnp.einsum('ugf,gif->ugi', value_shrinking_decay, backward_state_reduced, precision=maximum_precision)
        value_gradient = jnp.einsum('hts,thd->shd', scores, gradient_per_head, precision=maximum_precision)
        value_gradient = value_gradient + jnp.einsum('urf,rfa->ura', key_shrinking_decay, backward_state_reduced, precision=maximum_precision)
        block_backward_state = jnp.einsum('isx,isl->sxl', query_growing_decay, gradient_per_head, precision=maximum_precision)
        back_out = jnp.exp(totals)[:, None, None] * back_state + block_backward_state
        return (back_out, (query_gradient, key_gradient, value_gradient))
    _, (grad_q_all, grad_k_all, grad_v_all) = lax.scan(backward, zero_state, (query_all, key_all, value_all, cumulative, grad_att_all, states_low), reverse=True)

    def merge_heads(array):
        return array.reshape(TOKEN_COUNT, FEATURES).astype(jnp.bfloat16)
    return (normed_out, merge_heads(grad_q_all), merge_heads(grad_k_all), merge_heads(grad_v_all), gain_grad)
```

```python
import functools

import jax
import jax.numpy as jnp
from jax import lax
from jax.experimental import pallas as pl
from jax.experimental.pallas import tpu as pltpu
from jax.sharding import PartitionSpec as P

EPS = 1e-06
D = 128
LAG = 1
PIECES = 4
CUT = 2
LOG2E = 1.4426950408889634
MESH = pl.DeviceIdType.MESH
F32 = jnp.float32
BF16 = jnp.bfloat16


def mm(a, b, ca, cb):
    return lax.dot_general(a, b, (((ca,), (cb,)), ((), ())), preferred_element_type=F32)


def kernel(
    n_seq, n_head, heads, rows, features,
    q_hbm, k_hbm, v_hbm, dec_ref, gain_ref, og_hbm,
    no, gq, gk, gv, gg_ref,
    q, k, v, og, att, ga, st, ccol, crow, mask, mask_t, part, part2,
    send_f, recv_f, send_b, recv_b, acc_a, acc_p, inv, prj,
    stat, ggs, in_sem, fs_sem, fr_sem, bs_sem, br_sem,
    ss_sem, sr_sem, gs_sem, gr_sem,
):
    me = lax.axis_index("seq")
    mh = lax.axis_index("head")
    half = rows // 2

    def col(ref, h):
        return ref.at[:, pl.ds(pl.multiple_of(h * D, D), D)]

    loads = ((k_hbm, k), (v_hbm, v), (q_hbm, q), (og_hbm, og))

    def load(which, h):
        source, target = loads[which]
        return pltpu.make_async_copy(col(source, h), target.at[h], in_sem.at[which, h])

    def lanes(h):
        return pl.ds(pl.multiple_of(h * D, D), D)

    group = 2 if heads % 2 == 0 else 1

    def loads_of(pair):
        @pl.loop(0, heads)
        def _(h):
            for which in pair:
                load(which, h).start()

    barrier = pltpu.get_barrier_semaphore()

    @pl.when(me > 0)
    def _():
        pl.semaphore_signal(barrier, inc=1, device_id={"seq": lax.rem(me + n_seq - 1, n_seq)}, device_id_type=MESH)

    for d in range(1, n_head):
        pl.semaphore_signal(barrier, inc=1, device_id={"head": lax.rem(mh + d, n_head)}, device_id_type=MESH)

    loads_of((0, 1))

    upper = jnp.where(
        lax.broadcasted_iota(jnp.int32, (rows, rows), 0) <= lax.broadcasted_iota(jnp.int32, (rows, rows), 1), 1.0, 0.0
    ).astype(BF16)
    rest = dec_ref[...]
    sums = jnp.zeros_like(rest)
    for _ in range(3):
        piece = rest.astype(BF16)
        rest = rest - piece.astype(F32)
        sums = sums + mm(piece, upper, 1, 0)
    crow[...] = sums * LOG2E

    def prepare():
        loads_of((2, 3))
        down = lax.broadcasted_iota(jnp.int32, (half, half), 0)
        across = lax.broadcasted_iota(jnp.int32, (half, half), 1)
        mask[...] = jnp.where(down >= across, 0.0, -1e30)
        mask_t[...] = jnp.where(down <= across, 0.0, -1e30)
        acc_a[...] = jnp.zeros_like(acc_a)
        acc_p[...] = jnp.zeros_like(acc_p)

        @pl.when(me == 0)
        def _():
            recv_f[...] = jnp.zeros_like(recv_f)

        @pl.when(me == n_seq - 1)
        def _():
            recv_b[...] = jnp.zeros_like(recv_b)

    strip = D // CUT

    def forth(h, c):
        here = pl.ds(c * strip, strip)
        return pltpu.make_async_remote_copy(
            src_ref=send_f.at[h, here, :], dst_ref=recv_f.at[h, here, :],
            send_sem=fs_sem.at[h, c], recv_sem=fr_sem.at[h, c],
            device_id={"seq": lax.rem(me + 1, n_seq)}, device_id_type=MESH)

    def back(h, c):
        here = pl.ds(c * strip, strip)
        return pltpu.make_async_remote_copy(
            src_ref=send_b.at[h, here, :], dst_ref=recv_b.at[h, here, :],
            send_sem=bs_sem.at[h, c], recv_sem=br_sem.at[h, c],
            device_id={"seq": lax.rem(me + n_seq - 1, n_seq)}, device_id_type=MESH)

    def link(h, c, copy, sent, received, first, last):
        @pl.when(jnp.logical_not(first))
        def _():
            copy(h, c).wait_recv()

            @pl.when(jnp.logical_not(last))
            def _():
                here = pl.ds(c * strip, strip)
                decay = jnp.exp2(ccol[h, rows - 1:rows, :])
                sent[h, here, :] = decay * received[h, here, :] + sent[h, here, :]
                copy(h, c).start()

    def rising(h):
        return jnp.exp2(ccol[h])

    def falling(h):
        c = ccol[h]
        return jnp.exp2(c[rows - 1:rows] - c)

    def scaled(x, factor):
        return (x.astype(F32) * factor).astype(BF16)

    def own_states(i):
        some = [i * group + u for u in range(group)]
        for h in some:
            load(0, h).wait()
            load(1, h).wait()
        cols = [jnp.broadcast_to(crow[pl.ds(h, 1), :], (D, rows)).T for h in some]
        falls = [jnp.exp2(c[rows - 1:rows] - c) for c in cols]
        states = [mm(scaled(k[h], f), v[h], 0, 0) for h, f in zip(some, falls)]
        for h, c, state in zip(some, cols, states):
            ccol[h] = c
            send_f[h] = state

    def send_own(i):
        @pl.when((me == 0) & (n_seq > 1))
        def _():
            for u in range(group):
                for c in range(CUT):
                    forth(i * group + u, c).start()

    own_states(0)
    pl.semaphore_wait(barrier, n_head - 1 + jnp.where(me < n_seq - 1, 1, 0))
    send_own(0)
    prepare()

    @pl.loop(1, heads // group)
    def _(i):
        own_states(i)
        send_own(i)

    def wide(h, lo, hi, width):
        c = ccol[h, lo:hi, :]
        return jnp.concatenate([c] * (width // D), axis=1)

    def weigh(h, t, s, raw):
        spread = wide(h, t, t + half, half) - crow[pl.ds(h, 1), s:s + half]
        if s == t:
            spread = spread + mask[...]
        return (raw * jnp.exp2(spread)).astype(BF16)

    def weigh_t(h, s, t, raw):
        spread = crow[pl.ds(h, 1), t:t + half] - wide(h, s, s + half, half)
        if s == t:
            spread = spread + mask_t[...]
        return (raw * jnp.exp2(spread)).astype(BF16)

    def lower(h, a, b):
        a0, a1, b0, b1 = a[0:half], a[half:rows], b[0:half], b[half:rows]
        return (
            weigh(h, 0, 0, mm(a0, b0, 1, 1)),
            weigh(h, half, 0, mm(a1, b0, 1, 1)),
            weigh(h, half, half, mm(a1, b1, 1, 1)),
        )

    def upper_t(h, a, b):
        a0, a1, b0, b1 = a[0:half], a[half:rows], b[0:half], b[half:rows]
        return (
            weigh_t(h, 0, 0, mm(a0, b0, 1, 1)),
            weigh_t(h, 0, half, mm(a0, b1, 1, 1)),
            weigh_t(h, half, half, mm(a1, b1, 1, 1)),
        )

    def below(tiles, x):
        return mm(tiles[0], x[0:half], 1, 0), mm(tiles[1], x[0:half], 1, 0) + mm(tiles[2], x[half:rows], 1, 0)

    def above(tiles, x):
        return mm(tiles[0], x[0:half], 1, 0) + mm(tiles[1], x[half:rows], 1, 0), mm(tiles[2], x[half:rows], 1, 0)

    def inner(h):
        x, y = q[h], k[h]
        part[h, 0:half, :], part[h, half:rows, :] = below(lower(h, x, y), v[h])
        for n, tile in enumerate(upper_t(h, y, x)):
            st[h, n] = tile

    def outer(h):
        low = recv_f[h].astype(BF16)
        a = (part[h] + mm(scaled(q[h], rising(h)), low, 1, 0)).astype(BF16)
        att[h] = a
        a = a.astype(F32)
        acc_a[...] += a * a
        acc_p[...] += og[h].astype(F32) * gain_ref[pl.ds(h, 1), :] * a

    def skewed(lag, ready, inside, join, after):
        @pl.loop(0, lag)
        def _(i):
            ready(i)
            inside(i)

        @pl.loop(lag, heads)
        def _(i):
            ready(i)
            join(i - lag, 0)
            inside(i)
            for c in range(1, CUT):
                join(i - lag, c)
            after(i - lag)

        @pl.loop(heads - lag, heads)
        def _(i):
            for c in range(CUT):
                join(i, c)
            after(i)

    def ready_f(h):
        load(2, h).wait()
        load(3, h).wait()

    def join_f(h, c):
        link(h, c, forth, send_f, recv_f, me == 0, me == n_seq - 1)

    def join_b(h, c):
        link(h, c, back, send_b, recv_b, me == n_seq - 1, me == 0)
        if c == 0:
            @pl.when(h == 0)
            def _():
                for d in range(1, n_seq):
                    share_gain(d, me).start()

    skewed(jnp.minimum(LAG * me, heads), ready_f, inner, join_f, outer)

    stat[mh, 0:1, :] = jnp.sum(acc_a[...].T, axis=0, keepdims=True)
    stat[mh, 1:2, :] = jnp.sum(acc_p[...].T, axis=0, keepdims=True)

    def share_stat(d, slot):
        return pltpu.make_async_remote_copy(
            src_ref=stat.at[mh], dst_ref=stat.at[slot], send_sem=ss_sem.at[d], recv_sem=sr_sem.at[slot],
            device_id={"head": lax.rem(mh + d, n_head)}, device_id_type=MESH)

    for d in range(1, n_head):
        share_stat(d, mh).start()
    for d in range(1, n_head):
        share_stat(d, lax.rem(mh + d, n_head)).wait_recv()
    sums = stat[0]
    for j in range(1, n_head):
        sums = sums + stat[j]
    scale = lax.rsqrt(sums[0:1] / features + EPS)
    inv[...] = jnp.broadcast_to(scale, (D, rows)).T
    prj[...] = jnp.broadcast_to(scale * (sums[1:2] / features), (D, rows)).T

    @pl.loop(0, heads // group)
    def _(i):
        some = [i * group + u for u in range(group)]
        grads, states = [], []
        for h in some:
            g = gain_ref[pl.ds(h, 1), :]
            o = og[h].astype(F32)
            r = inv[...]
            normed = att[h].astype(F32) * r
            grad = (r * (o * g - normed * prj[...])).astype(BF16)
            states.append(mm(scaled(q[h], rising(h)), grad, 0, 0))
            grads.append((grad, (normed * g).astype(BF16), jnp.sum(o * normed, axis=0, keepdims=True)))
        for h, (grad, out, gain), state in zip(some, grads, states):
            send_b[h] = state
            ga[h] = grad
            no[:, lanes(h)] = out
            ggs[me, pl.ds(h, 1), :] = gain

        @pl.when((me == n_seq - 1) & (n_seq > 1))
        def _():
            for h in some:
                for c in range(CUT):
                    back(h, c).start()

    def share_gain(d, slot):
        return pltpu.make_async_remote_copy(
            src_ref=ggs.at[me], dst_ref=ggs.at[slot], send_sem=gs_sem.at[d], recv_sem=gr_sem.at[slot],
            device_id={"seq": lax.rem(me + d, n_seq)}, device_id_type=MESH)

    def inner_back(h):
        grad, x, y, z = ga[h], q[h], k[h], v[h]
        top, bottom = below(lower(h, grad, z), y)
        up = mm(scaled(grad, rising(h)), recv_f[h].astype(BF16), 1, 1)
        part[h, 0:half, :], part[h, half:rows, :] = above(upper_t(h, z, grad), x)
        part2[h, 0:half, :], part2[h, half:rows, :] = above([st[h, n] for n in range(3)], grad)
        gq[0:half, lanes(h)] = (top + up[0:half]).astype(BF16)
        gq[half:rows, lanes(h)] = (bottom + up[half:rows]).astype(BF16)

    def outer_back(h):
        low = recv_b[h].astype(BF16)
        fall = falling(h)
        gk[:, lanes(h)] = (part[h] + mm(scaled(v[h], fall), low, 1, 1)).astype(BF16)
        gv[:, lanes(h)] = (part2[h] + mm(scaled(k[h], fall), low, 1, 0)).astype(BF16)

    skewed(jnp.minimum(LAG * (n_seq - 1 - me), heads), lambda h: None, inner_back, join_b, outer_back)

    for d in range(1, n_seq):
        share_gain(d, lax.rem(me + d, n_seq)).wait_recv()
    total = ggs[0]
    for j in range(1, n_seq):
        total = total + ggs[j]
    gg_ref[...] = total

    for d in range(1, n_head):
        share_stat(d, mh).wait_send()
    for d in range(1, n_seq):
        share_gain(d, me).wait_send()

    @pl.loop(0, heads)
    def _(h):
        for c in range(CUT):
            @pl.when(me < n_seq - 1)
            def _():
                forth(h, c).wait_send()

            @pl.when(me > 0)
            def _():
                back(h, c).wait_send()


def store(heads, *refs):
    sources, targets, sem = refs[:5], refs[5:10], refs[10]
    copies = []
    for n, (source, target) in enumerate(zip(sources, targets)):
        parts = PIECES if n < 4 else 1
        size = source.shape[0] // parts
        for p in range(parts):
            here = pl.ds(p * size, size)
            copies.append(pltpu.make_async_copy(source.at[here, :], target.at[here, :], sem.at[n, p]))
    for copy in copies:
        copy.start()
    for copy in copies:
        copy.wait()


def local(n_seq, n_head, queries, key_vectors, values, decay_log, norm_gain, out_grad):
    rows, width = queries.shape
    heads = decay_log.shape[0]
    big = pltpu.VMEM((rows, width), BF16)
    hbm = pl.BlockSpec(memory_space=pl.ANY)
    vmem = pl.BlockSpec(memory_space=pltpu.VMEM)
    low = pltpu.VMEM((heads, rows, D), BF16)
    full = pltpu.VMEM((heads, rows, D), F32)
    state = pltpu.VMEM((heads, D, D), F32)
    plane = pltpu.VMEM((rows, D), F32)
    tile = pltpu.VMEM((rows // 2, rows // 2), F32)
    gain = jax.ShapeDtypeStruct((heads, D), F32)
    small = pltpu.VMEM((heads, D), F32)
    dma = pltpu.SemaphoreType.DMA
    outs = pl.pallas_call(
        functools.partial(kernel, n_seq, n_head, heads, rows, width * n_head),
        out_shape=(big, big, big, big, small),
        in_specs=[hbm, hbm, hbm, vmem, vmem, hbm],
        out_specs=(vmem, vmem, vmem, vmem, vmem),
        scratch_shapes=[
            low, low, low, low, low, low, pltpu.VMEM((heads, 3, rows // 2, rows // 2), BF16), full,
            pltpu.VMEM((heads, rows), F32), tile, tile, full, full,
            state, state, state, state, plane, plane, plane, plane,
            pltpu.VMEM((n_head, 2, rows), F32), pltpu.VMEM((n_seq, heads, D), F32),
            dma((4, heads)), dma((heads, CUT)), dma((heads, CUT)), dma((heads, CUT)), dma((heads, CUT)),
            dma((n_head,)), dma((n_head,)), dma((n_seq,)), dma((n_seq,)),
        ],
        compiler_params=pltpu.CompilerParams(
            collective_id=0, has_side_effects=True, vmem_limit_bytes=46 * 2**20),
    )(queries, key_vectors, values, decay_log, norm_gain.reshape(heads, D), out_grad)
    wide = jax.ShapeDtypeStruct((rows, width), BF16)
    outs = pl.pallas_call(
        functools.partial(store, heads),
        out_shape=(wide, wide, wide, wide, gain),
        in_specs=[vmem] * 5,
        out_specs=(hbm,) * 5,
        scratch_shapes=[dma((5, PIECES))],
        compiler_params=pltpu.CompilerParams(vmem_limit_bytes=2**20),
    )(*[pltpu.with_memory_space_constraint(out, pltpu.VMEM) for out in outs])
    return outs[:4] + (outs[4].reshape(heads * D),)


def solution(mesh):
    wide = P(("grp", "seq"), "head")
    return jax.shard_map(
        functools.partial(local, mesh.shape["seq"], mesh.shape["head"]),
        mesh=mesh,
        in_specs=(wide, wide, wide, P("head", ("grp", "seq")), P("head"), wide),
        out_specs=(wide, wide, wide, wide, P(("grp", "head"))),
        check_vma=False,
    )
```

```python
import functools

import jax
import jax.numpy as jnp
from jax import lax
from jax.experimental import pallas as pl
from jax.experimental.pallas import tpu as pltpu
from jax.sharding import PartitionSpec as P

EPS = 1e-06
D = 128
LAG = 1
PIECES = 4
CUT = 2
LEAD = 4
LOG2E = 1.4426950408889634
MESH = pl.DeviceIdType.MESH
F32 = jnp.float32
BF16 = jnp.bfloat16


def mm(a, b, ca, cb):
    return lax.dot_general(a, b, (((ca,), (cb,)), ((), ())), preferred_element_type=F32)


def kernel(
    n_seq, n_head, heads, rows, features,
    q_hbm, k_hbm, v_hbm, dec_ref, gain_ref, og_hbm,
    no, gq, gk, gv, gg_ref,
    q, k, v, og, att, ga, st, ccol, crow, mask, mask_t, part, part2,
    qr, send_f, recv_f, send_b, recv_b, acc_a, acc_p, inv, prj,
    stat, ggs, in_sem, fs_sem, fr_sem, bs_sem, br_sem,
    ss_sem, sr_sem, gs_sem, gr_sem,
):
    me = lax.axis_index("seq")
    mh = lax.axis_index("head")
    half = rows // 2

    def col(ref, h):
        return ref.at[:, pl.ds(pl.multiple_of(h * D, D), D)]

    loads = ((k_hbm, k), (v_hbm, v), (q_hbm, q), (og_hbm, og))

    def load(which, h):
        source, target = loads[which]
        return pltpu.make_async_copy(col(source, h), target.at[h], in_sem.at[which, h])

    def lanes(h):
        return pl.ds(pl.multiple_of(h * D, D), D)

    group = 2 if heads % 2 == 0 else 1

    def loads_of(pair):
        @pl.loop(0, heads)
        def _(h):
            for which in pair:
                load(which, h).start()

    barrier = pltpu.get_barrier_semaphore()

    @pl.when(me > 0)
    def _():
        pl.semaphore_signal(barrier, inc=1, device_id={"seq": lax.rem(me + n_seq - 1, n_seq)}, device_id_type=MESH)

    for d in range(1, n_head):
        pl.semaphore_signal(barrier, inc=1, device_id={"head": lax.rem(mh + d, n_head)}, device_id_type=MESH)

    loads_of((0, 1))

    upper = jnp.where(
        lax.broadcasted_iota(jnp.int32, (rows, rows), 0) <= lax.broadcasted_iota(jnp.int32, (rows, rows), 1), 1.0, 0.0
    ).astype(BF16)
    rest = dec_ref[...]
    sums = jnp.zeros_like(rest)
    for _ in range(3):
        piece = rest.astype(BF16)
        rest = rest - piece.astype(F32)
        sums = sums + mm(piece, upper, 1, 0)
    crow[...] = sums * LOG2E

    def prepare():
        loads_of((2, 3))
        down = lax.broadcasted_iota(jnp.int32, (half, half), 0)
        across = lax.broadcasted_iota(jnp.int32, (half, half), 1)
        mask[...] = jnp.where(down >= across, 0.0, -1e30)
        mask_t[...] = jnp.where(down <= across, 0.0, -1e30)
        acc_a[...] = jnp.zeros_like(acc_a)
        acc_p[...] = jnp.zeros_like(acc_p)

        @pl.when(me == 0)
        def _():
            recv_f[...] = jnp.zeros_like(recv_f)

        @pl.when(me == n_seq - 1)
        def _():
            recv_b[...] = jnp.zeros_like(recv_b)

    strip = D // CUT

    def forth(h, c):
        here = pl.ds(c * strip, strip)
        return pltpu.make_async_remote_copy(
            src_ref=send_f.at[h, here, :], dst_ref=recv_f.at[h, here, :],
            send_sem=fs_sem.at[h, c], recv_sem=fr_sem.at[h, c],
            device_id={"seq": lax.rem(me + 1, n_seq)}, device_id_type=MESH)

    def back(h, c):
        here = pl.ds(c * strip, strip)
        return pltpu.make_async_remote_copy(
            src_ref=send_b.at[h, here, :], dst_ref=recv_b.at[h, here, :],
            send_sem=bs_sem.at[h, c], recv_sem=br_sem.at[h, c],
            device_id={"seq": lax.rem(me + n_seq - 1, n_seq)}, device_id_type=MESH)

    def link(h, c, copy, sent, received, first, last):
        @pl.when(jnp.logical_not(first))
        def _():
            here = pl.ds(c * strip, strip)
            decay = jnp.exp2(ccol[h, rows - 1:rows, :])
            copy(h, c).wait_recv()

            @pl.when(jnp.logical_not(last))
            def _():
                sent[h, here, :] = decay * received[h, here, :] + sent[h, here, :]
                copy(h, c).start()

    def rising(h):
        return jnp.exp2(ccol[h])

    def falling(h):
        c = ccol[h]
        return jnp.exp2(c[rows - 1:rows] - c)

    def scaled(x, factor):
        return (x.astype(F32) * factor).astype(BF16)

    def own_states(i):
        some = [i * group + u for u in range(group)]
        for h in some:
            load(0, h).wait()
            load(1, h).wait()
        cols = [jnp.broadcast_to(crow[pl.ds(h, 1), :], (D, rows)).T for h in some]
        falls = [jnp.exp2(c[rows - 1:rows] - c) for c in cols]
        states = [mm(scaled(k[h], f), v[h], 0, 0) for h, f in zip(some, falls)]
        for h, c, state in zip(some, cols, states):
            ccol[h] = c
            send_f[h] = state

    def send_own(i):
        @pl.when((me == 0) & (n_seq > 1))
        def _():
            for u in range(group):
                for c in range(CUT):
                    forth(i * group + u, c).start()

    own_states(0)
    pl.semaphore_wait(barrier, n_head - 1 + jnp.where(me < n_seq - 1, 1, 0))
    send_own(0)
    prepare()

    groups = heads // group
    lead = jnp.where(me == 1, min(LEAD, groups), groups)

    @pl.loop(1, lead)
    def _(i):
        own_states(i)
        send_own(i)

    def wide(h, lo, hi, width):
        c = ccol[h, lo:hi, :]
        return jnp.concatenate([c] * (width // D), axis=1)

    def weigh(h, t, s, raw):
        spread = wide(h, t, t + half, half) - crow[pl.ds(h, 1), s:s + half]
        if s == t:
            spread = spread + mask[...]
        return (raw * jnp.exp2(spread)).astype(BF16)

    def weigh_t(h, s, t, raw):
        spread = crow[pl.ds(h, 1), t:t + half] - wide(h, s, s + half, half)
        if s == t:
            spread = spread + mask_t[...]
        return (raw * jnp.exp2(spread)).astype(BF16)

    def lower(h, a, b):
        a0, a1, b0, b1 = a[0:half], a[half:rows], b[0:half], b[half:rows]
        return (
            weigh(h, 0, 0, mm(a0, b0, 1, 1)),
            weigh(h, half, 0, mm(a1, b0, 1, 1)),
            weigh(h, half, half, mm(a1, b1, 1, 1)),
        )

    def upper_t(h, a, b):
        a0, a1, b0, b1 = a[0:half], a[half:rows], b[0:half], b[half:rows]
        return (
            weigh_t(h, 0, 0, mm(a0, b0, 1, 1)),
            weigh_t(h, 0, half, mm(a0, b1, 1, 1)),
            weigh_t(h, half, half, mm(a1, b1, 1, 1)),
        )

    def below(tiles, x):
        return mm(tiles[0], x[0:half], 1, 0), mm(tiles[1], x[0:half], 1, 0) + mm(tiles[2], x[half:rows], 1, 0)

    def above(tiles, x):
        return mm(tiles[0], x[0:half], 1, 0) + mm(tiles[1], x[half:rows], 1, 0), mm(tiles[2], x[half:rows], 1, 0)

    def inner(h):
        x, y = q[h], k[h]
        qr[h] = scaled(x, rising(h))
        part[h, 0:half, :], part[h, half:rows, :] = below(lower(h, x, y), v[h])
        for n, tile in enumerate(upper_t(h, y, x)):
            st[h, n] = tile

    def outer(h):
        low = recv_f[h].astype(BF16)
        a = (part[h] + mm(qr[h], low, 1, 0)).astype(BF16)
        att[h] = a
        a = a.astype(F32)
        acc_a[...] += a * a
        acc_p[...] += og[h].astype(F32) * gain_ref[pl.ds(h, 1), :] * a

    def skewed(lag, more, ready, inside, join, after):
        @pl.loop(0, lag)
        def _(i):
            ready(i)
            inside(i)

        @pl.loop(lag, heads)
        def _(i):
            more(i)
            ready(i)
            join(i - lag, 0)
            inside(i)
            for c in range(1, CUT):
                join(i - lag, c)
            after(i - lag)

        @pl.loop(heads - lag, heads)
        def _(i):
            for c in range(CUT):
                join(i, c)
            after(i)

    def ready_f(h):
        load(2, h).wait()
        load(3, h).wait()

    def more_f(h):
        at = h // group + lead

        @pl.when((h % group == 0) & (at < groups))
        def _():
            own_states(at)

    def join_f(h, c):
        link(h, c, forth, send_f, recv_f, me == 0, me == n_seq - 1)

    def join_b(h, c):
        link(h, c, back, send_b, recv_b, me == n_seq - 1, me == 0)
        if c == 0:
            @pl.when(h == 0)
            def _():
                for d in range(1, n_seq):
                    share_gain(d, me).start()

    skewed(jnp.clip(LAG * (me - 1), 0, heads), more_f, ready_f, inner, join_f, outer)

    stat[mh, 0:1, :] = jnp.sum(acc_a[...].T, axis=0, keepdims=True)
    stat[mh, 1:2, :] = jnp.sum(acc_p[...].T, axis=0, keepdims=True)

    def share_stat(d, slot):
        return pltpu.make_async_remote_copy(
            src_ref=stat.at[mh], dst_ref=stat.at[slot], send_sem=ss_sem.at[d], recv_sem=sr_sem.at[slot],
            device_id={"head": lax.rem(mh + d, n_head)}, device_id_type=MESH)

    for d in range(1, n_head):
        share_stat(d, mh).start()
    for d in range(1, n_head):
        share_stat(d, lax.rem(mh + d, n_head)).wait_recv()
    sums = stat[0]
    for j in range(1, n_head):
        sums = sums + stat[j]
    scale = lax.rsqrt(sums[0:1] / features + EPS)
    inv[...] = jnp.broadcast_to(scale, (D, rows)).T
    prj[...] = jnp.broadcast_to(scale * (sums[1:2] / features), (D, rows)).T

    @pl.loop(0, heads // group)
    def _(i):
        some = [i * group + u for u in range(group)]
        grads, states = [], []
        for h in some:
            g = gain_ref[pl.ds(h, 1), :]
            o = og[h].astype(F32)
            r = inv[...]
            normed = att[h].astype(F32) * r
            grad = (r * (o * g - normed * prj[...])).astype(BF16)
            states.append(mm(qr[h], grad, 0, 0))
            grads.append((grad, (normed * g).astype(BF16), jnp.sum(o * normed, axis=0, keepdims=True)))
        for h, (grad, out, gain), state in zip(some, grads, states):
            send_b[h] = state
            ga[h] = grad
            no[:, lanes(h)] = out
            ggs[me, pl.ds(h, 1), :] = gain

        @pl.when((me == n_seq - 1) & (n_seq > 1))
        def _():
            for h in some:
                for c in range(CUT):
                    back(h, c).start()

    def share_gain(d, slot):
        return pltpu.make_async_remote_copy(
            src_ref=ggs.at[me], dst_ref=ggs.at[slot], send_sem=gs_sem.at[d], recv_sem=gr_sem.at[slot],
            device_id={"seq": lax.rem(me + d, n_seq)}, device_id_type=MESH)

    def inner_back(h):
        grad, x, y, z = ga[h], q[h], k[h], v[h]
        top, bottom = below(lower(h, grad, z), y)
        up = mm(scaled(grad, rising(h)), recv_f[h].astype(BF16), 1, 1)
        part[h, 0:half, :], part[h, half:rows, :] = above(upper_t(h, z, grad), x)
        part2[h, 0:half, :], part2[h, half:rows, :] = above([st[h, n] for n in range(3)], grad)
        gq[0:half, lanes(h)] = (top + up[0:half]).astype(BF16)
        gq[half:rows, lanes(h)] = (bottom + up[half:rows]).astype(BF16)

    def outer_back(h):
        low = recv_b[h].astype(BF16)
        fall = falling(h)
        gk[:, lanes(h)] = (part[h] + mm(scaled(v[h], fall), low, 1, 1)).astype(BF16)
        gv[:, lanes(h)] = (part2[h] + mm(scaled(k[h], fall), low, 1, 0)).astype(BF16)

    skewed(jnp.clip(LAG * (n_seq - 2 - me), 0, heads), lambda h: None, lambda h: None, inner_back, join_b, outer_back)

    for d in range(1, n_seq):
        share_gain(d, lax.rem(me + d, n_seq)).wait_recv()
    total = ggs[0]
    for j in range(1, n_seq):
        total = total + ggs[j]
    gg_ref[...] = total

    for d in range(1, n_head):
        share_stat(d, mh).wait_send()
    for d in range(1, n_seq):
        share_gain(d, me).wait_send()

    @pl.loop(0, heads)
    def _(h):
        for c in range(CUT):
            @pl.when(me < n_seq - 1)
            def _():
                forth(h, c).wait_send()

            @pl.when(me > 0)
            def _():
                back(h, c).wait_send()


def store(heads, *refs):
    sources, targets, sem = refs[:5], refs[5:10], refs[10]
    copies = []
    for n, (source, target) in enumerate(zip(sources, targets)):
        parts = PIECES if n < 4 else 1
        size = source.shape[0] // parts
        for p in range(parts):
            here = pl.ds(p * size, size)
            copies.append(pltpu.make_async_copy(source.at[here, :], target.at[here, :], sem.at[n, p]))
    for copy in copies:
        copy.start()
    for copy in copies:
        copy.wait()


def local(n_seq, n_head, queries, key_vectors, values, decay_log, norm_gain, out_grad):
    rows, width = queries.shape
    heads = decay_log.shape[0]
    big = pltpu.VMEM((rows, width), BF16)
    hbm = pl.BlockSpec(memory_space=pl.ANY)
    vmem = pl.BlockSpec(memory_space=pltpu.VMEM)
    low = pltpu.VMEM((heads, rows, D), BF16)
    full = pltpu.VMEM((heads, rows, D), F32)
    state = pltpu.VMEM((heads, D, D), F32)
    plane = pltpu.VMEM((rows, D), F32)
    tile = pltpu.VMEM((rows // 2, rows // 2), F32)
    gain = jax.ShapeDtypeStruct((heads, D), F32)
    small = pltpu.VMEM((heads, D), F32)
    dma = pltpu.SemaphoreType.DMA
    outs = pl.pallas_call(
        functools.partial(kernel, n_seq, n_head, heads, rows, width * n_head),
        out_shape=(big, big, big, big, small),
        in_specs=[hbm, hbm, hbm, vmem, vmem, hbm],
        out_specs=(vmem, vmem, vmem, vmem, vmem),
        scratch_shapes=[
            low, low, low, low, low, low, pltpu.VMEM((heads, 3, rows // 2, rows // 2), BF16), full,
            pltpu.VMEM((heads, rows), F32), tile, tile, full, full,
            low, state, state, state, state, plane, plane, plane, plane,
            pltpu.VMEM((n_head, 2, rows), F32), pltpu.VMEM((n_seq, heads, D), F32),
            dma((4, heads)), dma((heads, CUT)), dma((heads, CUT)), dma((heads, CUT)), dma((heads, CUT)),
            dma((n_head,)), dma((n_head,)), dma((n_seq,)), dma((n_seq,)),
        ],
        compiler_params=pltpu.CompilerParams(
            collective_id=0, has_side_effects=True, vmem_limit_bytes=50 * 2**20),
    )(queries, key_vectors, values, decay_log, norm_gain.reshape(heads, D), out_grad)
    wide = jax.ShapeDtypeStruct((rows, width), BF16)
    outs = pl.pallas_call(
        functools.partial(store, heads),
        out_shape=(wide, wide, wide, wide, gain),
        in_specs=[vmem] * 5,
        out_specs=(hbm,) * 5,
        scratch_shapes=[dma((5, PIECES))],
        compiler_params=pltpu.CompilerParams(vmem_limit_bytes=2**20),
    )(*[pltpu.with_memory_space_constraint(out, pltpu.VMEM) for out in outs])
    return outs[:4] + (outs[4].reshape(heads * D),)


def solution(mesh):
    wide = P(("grp", "seq"), "head")
    return jax.shard_map(
        functools.partial(local, mesh.shape["seq"], mesh.shape["head"]),
        mesh=mesh,
        in_specs=(wide, wide, wide, P("head", ("grp", "seq")), P("head"), wide),
        out_specs=(wide, wide, wide, wide, P(("grp", "head"))),
        check_vma=False,
    )
```

```python
import functools

import jax
import jax.numpy as jnp
from jax import lax
from jax.experimental import pallas as pl
from jax.experimental.pallas import tpu as pltpu
from jax.sharding import PartitionSpec as P

EPS = 1e-06
D = 128
LAG_F = 2
LAG_B = 4
PIECES = 4
CUT = 2
LEAD = 3
LOG2E = 1.4426950408889634
MESH = pl.DeviceIdType.MESH
F32 = jnp.float32
BF16 = jnp.bfloat16


def mm(a, b, ca, cb):
    return lax.dot_general(a, b, (((ca,), (cb,)), ((), ())), preferred_element_type=F32)


def kernel(
    n_seq, n_head, heads, rows, features,
    q_hbm, k_hbm, v_hbm, dec_ref, gain_ref, og_hbm,
    no, gq, gk, gv, gg_ref,
    q, k, v, og, att, ga, st, ccol, crow, mask, mask_t, part, part2,
    qr, send_f, recv_f, send_b, recv_b, acc_a, acc_p, inv, prj,
    stat, ggs, in_sem, fs_sem, fr_sem, bs_sem, br_sem,
    ss_sem, sr_sem, gs_sem, gr_sem,
):
    me = lax.axis_index("seq")
    mh = lax.axis_index("head")
    half = rows // 2

    def col(ref, h):
        return ref.at[:, pl.ds(pl.multiple_of(h * D, D), D)]

    loads = ((k_hbm, k), (v_hbm, v), (q_hbm, q), (og_hbm, og))

    def load(which, h):
        source, target = loads[which]
        return pltpu.make_async_copy(col(source, h), target.at[h], in_sem.at[which, h])

    def lanes(h):
        return pl.ds(pl.multiple_of(h * D, D), D)

    group = 2 if heads % 2 == 0 else 1

    def loads_of(pair):
        @pl.loop(0, heads)
        def _(h):
            for which in pair:
                load(which, h).start()

    barrier = pltpu.get_barrier_semaphore()

    @pl.when(me > 0)
    def _():
        pl.semaphore_signal(barrier, inc=1, device_id={"seq": lax.rem(me + n_seq - 1, n_seq)}, device_id_type=MESH)

    for d in range(1, n_head):
        pl.semaphore_signal(barrier, inc=1, device_id={"head": lax.rem(mh + d, n_head)}, device_id_type=MESH)

    loads_of((0, 1))

    upper = jnp.where(
        lax.broadcasted_iota(jnp.int32, (rows, rows), 0) <= lax.broadcasted_iota(jnp.int32, (rows, rows), 1), 1.0, 0.0
    ).astype(BF16)
    rest = dec_ref[...]
    sums = jnp.zeros_like(rest)
    for _ in range(3):
        piece = rest.astype(BF16)
        rest = rest - piece.astype(F32)
        sums = sums + mm(piece, upper, 1, 0)
    crow[...] = sums * LOG2E

    def prepare():
        loads_of((2, 3))
        down = lax.broadcasted_iota(jnp.int32, (half, half), 0)
        across = lax.broadcasted_iota(jnp.int32, (half, half), 1)
        mask[...] = jnp.where(down >= across, 0.0, -1e30)
        mask_t[...] = jnp.where(down <= across, 0.0, -1e30)
        acc_a[...] = jnp.zeros_like(acc_a)
        acc_p[...] = jnp.zeros_like(acc_p)

        @pl.when(me == 0)
        def _():
            recv_f[...] = jnp.zeros_like(recv_f)

        @pl.when(me == n_seq - 1)
        def _():
            recv_b[...] = jnp.zeros_like(recv_b)

    strip = D // CUT

    def forth(h, c):
        here = pl.ds(c * strip, strip)
        return pltpu.make_async_remote_copy(
            src_ref=send_f.at[h, here, :], dst_ref=recv_f.at[h, here, :],
            send_sem=fs_sem.at[h, c], recv_sem=fr_sem.at[h, c],
            device_id={"seq": lax.rem(me + 1, n_seq)}, device_id_type=MESH)

    def back(h, c):
        here = pl.ds(c * strip, strip)
        return pltpu.make_async_remote_copy(
            src_ref=send_b.at[h, here, :], dst_ref=recv_b.at[h, here, :],
            send_sem=bs_sem.at[h, c], recv_sem=br_sem.at[h, c],
            device_id={"seq": lax.rem(me + n_seq - 1, n_seq)}, device_id_type=MESH)

    def link(h, c, copy, sent, received, first, last):
        @pl.when(jnp.logical_not(first))
        def _():
            here = pl.ds(c * strip, strip)
            decay = jnp.exp2(ccol[h, rows - 1:rows, :])
            copy(h, c).wait_recv()

            @pl.when(jnp.logical_not(last))
            def _():
                sent[h, here, :] = decay * received[h, here, :] + sent[h, here, :]
                copy(h, c).start()

    def rising(h):
        return jnp.exp2(ccol[h])

    def falling(h):
        c = ccol[h]
        return jnp.exp2(c[rows - 1:rows] - c)

    def scaled(x, factor):
        return (x.astype(F32) * factor).astype(BF16)

    def own_states(i):
        some = [i * group + u for u in range(group)]
        for h in some:
            load(0, h).wait()
            load(1, h).wait()
        cols = [jnp.broadcast_to(crow[pl.ds(h, 1), :], (D, rows)).T for h in some]
        falls = [jnp.exp2(c[rows - 1:rows] - c) for c in cols]
        states = [mm(scaled(k[h], f), v[h], 0, 0) for h, f in zip(some, falls)]
        for h, c, state in zip(some, cols, states):
            ccol[h] = c
            send_f[h] = state

    def send_own(i):
        @pl.when((me == 0) & (n_seq > 1))
        def _():
            for u in range(group):
                for c in range(CUT):
                    forth(i * group + u, c).start()

    own_states(0)
    pl.semaphore_wait(barrier, n_head - 1 + jnp.where(me < n_seq - 1, 1, 0))
    send_own(0)
    prepare()

    groups = heads // group
    lead = jnp.where(me == 1, min(LEAD, groups), groups)

    @pl.loop(1, lead)
    def _(i):
        own_states(i)
        send_own(i)

    def wide(h, lo, hi, width):
        c = ccol[h, lo:hi, :]
        return jnp.concatenate([c] * (width // D), axis=1)

    def weigh(h, t, s, raw):
        spread = wide(h, t, t + half, half) - crow[pl.ds(h, 1), s:s + half]
        if s == t:
            spread = spread + mask[...]
        return (raw * jnp.exp2(spread)).astype(BF16)

    def weigh_t(h, s, t, raw):
        spread = crow[pl.ds(h, 1), t:t + half] - wide(h, s, s + half, half)
        if s == t:
            spread = spread + mask_t[...]
        return (raw * jnp.exp2(spread)).astype(BF16)

    def lower(h, a, b):
        a0, a1, b0, b1 = a[0:half], a[half:rows], b[0:half], b[half:rows]
        return (
            weigh(h, 0, 0, mm(a0, b0, 1, 1)),
            weigh(h, half, 0, mm(a1, b0, 1, 1)),
            weigh(h, half, half, mm(a1, b1, 1, 1)),
        )

    def upper_t(h, a, b):
        a0, a1, b0, b1 = a[0:half], a[half:rows], b[0:half], b[half:rows]
        return (
            weigh_t(h, 0, 0, mm(a0, b0, 1, 1)),
            weigh_t(h, 0, half, mm(a0, b1, 1, 1)),
            weigh_t(h, half, half, mm(a1, b1, 1, 1)),
        )

    def below(tiles, x):
        return mm(tiles[0], x[0:half], 1, 0), mm(tiles[1], x[0:half], 1, 0) + mm(tiles[2], x[half:rows], 1, 0)

    def above(tiles, x):
        return mm(tiles[0], x[0:half], 1, 0) + mm(tiles[1], x[half:rows], 1, 0), mm(tiles[2], x[half:rows], 1, 0)

    def inner(h):
        x, y = q[h], k[h]
        qr[h] = scaled(x, rising(h))
        part[h, 0:half, :], part[h, half:rows, :] = below(lower(h, x, y), v[h])
        for n, tile in enumerate(upper_t(h, y, x)):
            st[h, n] = tile

    def outer(h):
        low = recv_f[h].astype(BF16)
        a = (part[h] + mm(qr[h], low, 1, 0)).astype(BF16)
        att[h] = a
        a = a.astype(F32)
        acc_a[...] += a * a
        acc_p[...] += og[h].astype(F32) * gain_ref[pl.ds(h, 1), :] * a

    def skewed(lag, more, ready, inside, join, after):
        @pl.loop(0, lag)
        def _(i):
            ready(i)
            inside(i)

        @pl.loop(lag, heads)
        def _(i):
            more(i)
            ready(i)
            join(i - lag, 0)
            inside(i)
            for c in range(1, CUT):
                join(i - lag, c)
            after(i - lag)

        @pl.loop(heads - lag, heads)
        def _(i):
            for c in range(CUT):
                join(i, c)
            after(i)

    def ready_f(h):
        load(2, h).wait()
        load(3, h).wait()

    def more_f(h):
        at = h // group + lead

        @pl.when((h % group == 0) & (at < groups))
        def _():
            own_states(at)

    def join_f(h, c):
        link(h, c, forth, send_f, recv_f, me == 0, me == n_seq - 1)

    def join_b(h, c):
        if c == 0:
            @pl.when((me == 0) & (h == heads - 1))
            def _():
                gather_gain()

        link(h, c, back, send_b, recv_b, me == n_seq - 1, me == 0)
        if c == 0:
            @pl.when(h == 0)
            def _():
                for d in range(1, n_seq):
                    share_gain(d, me).start()

    skewed(jnp.clip(LAG_F * (me - 1), 0, heads), more_f, ready_f, inner, join_f, outer)

    stat[mh, 0:1, :] = jnp.sum(acc_a[...].T, axis=0, keepdims=True)
    stat[mh, 1:2, :] = jnp.sum(acc_p[...].T, axis=0, keepdims=True)

    def share_stat(d, slot):
        return pltpu.make_async_remote_copy(
            src_ref=stat.at[mh], dst_ref=stat.at[slot], send_sem=ss_sem.at[d], recv_sem=sr_sem.at[slot],
            device_id={"head": lax.rem(mh + d, n_head)}, device_id_type=MESH)

    for d in range(1, n_head):
        share_stat(d, mh).start()
    for d in range(1, n_head):
        share_stat(d, lax.rem(mh + d, n_head)).wait_recv()
    sums = stat[0]
    for j in range(1, n_head):
        sums = sums + stat[j]
    scale = lax.rsqrt(sums[0:1] / features + EPS)
    inv[...] = jnp.broadcast_to(scale, (D, rows)).T
    prj[...] = jnp.broadcast_to(scale * (sums[1:2] / features), (D, rows)).T

    @pl.loop(0, heads // group)
    def _(i):
        some = [i * group + u for u in range(group)]
        grads, states = [], []
        for h in some:
            g = gain_ref[pl.ds(h, 1), :]
            o = og[h].astype(F32)
            r = inv[...]
            normed = att[h].astype(F32) * r
            grad = (r * (o * g - normed * prj[...])).astype(BF16)
            states.append(mm(qr[h], grad, 0, 0))
            grads.append((grad, (normed * g).astype(BF16), jnp.sum(o * normed, axis=0, keepdims=True)))
        for h, state in zip(some, states):
            send_b[h] = state

        @pl.when((me == n_seq - 1) & (n_seq > 1))
        def _():
            for h in some:
                for c in range(CUT):
                    back(h, c).start()

        for h, (grad, out, gain) in zip(some, grads):
            ga[h] = grad
            no[:, lanes(h)] = out
            ggs[me, pl.ds(h, 1), :] = gain

    def share_gain(d, slot):
        return pltpu.make_async_remote_copy(
            src_ref=ggs.at[me], dst_ref=ggs.at[slot], send_sem=gs_sem.at[d], recv_sem=gr_sem.at[slot],
            device_id={"seq": lax.rem(me + d, n_seq)}, device_id_type=MESH)

    def gather_gain():
        for d in range(1, n_seq):
            share_gain(d, lax.rem(me + d, n_seq)).wait_recv()
        total = ggs[0]
        for j in range(1, n_seq):
            total = total + ggs[j]
        gg_ref[...] = total
        for d in range(1, n_seq):
            share_gain(d, me).wait_send()

    @pl.when(me < n_seq - 1)
    def _():
        @pl.loop(0, heads)
        def _(h):
            for c in range(CUT):
                forth(h, c).wait_send()

    for d in range(1, n_head):
        share_stat(d, mh).wait_send()

    def inner_back(h):
        grad, x, y, z = ga[h], q[h], k[h], v[h]
        top, bottom = below(lower(h, grad, z), y)
        up = mm(scaled(grad, rising(h)), recv_f[h].astype(BF16), 1, 1)
        part[h, 0:half, :], part[h, half:rows, :] = above(upper_t(h, z, grad), x)
        part2[h, 0:half, :], part2[h, half:rows, :] = above([st[h, n] for n in range(3)], grad)
        gq[0:half, lanes(h)] = (top + up[0:half]).astype(BF16)
        gq[half:rows, lanes(h)] = (bottom + up[half:rows]).astype(BF16)
        fall = falling(h)
        k[h] = scaled(y, fall)
        v[h] = scaled(z, fall)

    def outer_back(h):
        low = recv_b[h].astype(BF16)
        gk[:, lanes(h)] = (part[h] + mm(v[h], low, 1, 1)).astype(BF16)
        gv[:, lanes(h)] = (part2[h] + mm(k[h], low, 1, 0)).astype(BF16)

    skewed(jnp.clip(LAG_B * (n_seq - 2 - me), 0, heads), lambda h: None, lambda h: None, inner_back, join_b, outer_back)

    @pl.when(me > 0)
    def _():
        gather_gain()

        @pl.loop(0, heads)
        def _(h):
            for c in range(CUT):
                back(h, c).wait_send()


def store(heads, *refs):
    sources, targets, sem = refs[:5], refs[5:10], refs[10]
    copies = []
    for n, (source, target) in enumerate(zip(sources, targets)):
        parts = PIECES if n < 4 else 1
        size = source.shape[0] // parts
        for p in range(parts):
            here = pl.ds(p * size, size)
            copies.append(pltpu.make_async_copy(source.at[here, :], target.at[here, :], sem.at[n, p]))
    for copy in copies:
        copy.start()
    for copy in copies:
        copy.wait()


def local(n_seq, n_head, queries, key_vectors, values, decay_log, norm_gain, out_grad):
    rows, width = queries.shape
    heads = decay_log.shape[0]
    big = pltpu.VMEM((rows, width), BF16)
    hbm = pl.BlockSpec(memory_space=pl.ANY)
    vmem = pl.BlockSpec(memory_space=pltpu.VMEM)
    low = pltpu.VMEM((heads, rows, D), BF16)
    full = pltpu.VMEM((heads, rows, D), F32)
    state = pltpu.VMEM((heads, D, D), F32)
    plane = pltpu.VMEM((rows, D), F32)
    tile = pltpu.VMEM((rows // 2, rows // 2), F32)
    gain = jax.ShapeDtypeStruct((heads, D), F32)
    small = pltpu.VMEM((heads, D), F32)
    dma = pltpu.SemaphoreType.DMA
    outs = pl.pallas_call(
        functools.partial(kernel, n_seq, n_head, heads, rows, width * n_head),
        out_shape=(big, big, big, big, small),
        in_specs=[hbm, hbm, hbm, vmem, vmem, hbm],
        out_specs=(vmem, vmem, vmem, vmem, vmem),
        scratch_shapes=[
            low, low, low, low, low, low, pltpu.VMEM((heads, 3, rows // 2, rows // 2), BF16), full,
            pltpu.VMEM((heads, rows), F32), tile, tile, full, full,
            low, state, state, state, state, plane, plane, plane, plane,
            pltpu.VMEM((n_head, 2, rows), F32), pltpu.VMEM((n_seq, heads, D), F32),
            dma((4, heads)), dma((heads, CUT)), dma((heads, CUT)), dma((heads, CUT)), dma((heads, CUT)),
            dma((n_head,)), dma((n_head,)), dma((n_seq,)), dma((n_seq,)),
        ],
        compiler_params=pltpu.CompilerParams(
            collective_id=0, has_side_effects=True, vmem_limit_bytes=50 * 2**20),
    )(queries, key_vectors, values, decay_log, norm_gain.reshape(heads, D), out_grad)
    wide = jax.ShapeDtypeStruct((rows, width), BF16)
    outs = pl.pallas_call(
        functools.partial(store, heads),
        out_shape=(wide, wide, wide, wide, gain),
        in_specs=[vmem] * 5,
        out_specs=(hbm,) * 5,
        scratch_shapes=[dma((5, PIECES))],
        compiler_params=pltpu.CompilerParams(vmem_limit_bytes=2**20),
    )(*[pltpu.with_memory_space_constraint(out, pltpu.VMEM) for out in outs])
    return outs[:4] + (outs[4].reshape(heads * D),)


def solution(mesh):
    wide = P(("grp", "seq"), "head")
    return jax.shard_map(
        functools.partial(local, mesh.shape["seq"], mesh.shape["head"]),
        mesh=mesh,
        in_specs=(wide, wide, wide, P("head", ("grp", "seq")), P("head"), wide),
        out_specs=(wide, wide, wide, wide, P(("grp", "head"))),
        check_vma=False,
    )
```

```python
import functools

import jax
import jax.numpy as jnp
from jax import lax
from jax.experimental import pallas as pl
from jax.experimental.pallas import tpu as pltpu
from jax.sharding import PartitionSpec as P

EPS = 1e-06
D = 128
LAG_F = 2
LAG_B = 3
PIECES = 4
CUT = 2
LEAD = 4
HOLD_F = 15
LOG2E = 1.4426950408889634
MESH = pl.DeviceIdType.MESH
F32 = jnp.float32
BF16 = jnp.bfloat16


def mm(a, b, ca, cb):
    return lax.dot_general(a, b, (((ca,), (cb,)), ((), ())), preferred_element_type=F32)


def kernel(
    n_seq, n_head, heads, rows, features,
    q_hbm, k_hbm, v_hbm, dec_ref, gain_ref, og_hbm,
    no, gq, gk, gv, gg_ref,
    q, k, v, og, att, ga, st, ccol, crow, mask, mask_t, part, part2,
    qr, send_f, recv_f, send_b, recv_b, acc_a, acc_p, inv, prj,
    stat, ggs, in_sem, fs_sem, fr_sem, bs_sem, br_sem,
    ss_sem, sr_sem, gs_sem, gr_sem,
):
    me = lax.axis_index("seq")
    mh = lax.axis_index("head")
    half = rows // 2
    odd = lax.rem(mh, 2) == 1

    def col(ref, h):
        return ref.at[:, pl.ds(pl.multiple_of(h * D, D), D)]

    loads = ((k_hbm, k), (v_hbm, v), (q_hbm, q), (og_hbm, og))

    def load(which, h):
        source, target = loads[which]
        return pltpu.make_async_copy(col(source, h), target.at[h], in_sem.at[which, h])

    def lanes(h):
        return pl.ds(pl.multiple_of(h * D, D), D)

    group = 2 if heads % 2 == 0 else 1

    def loads_of(pair):
        @pl.loop(0, heads)
        def _(h):
            for which in pair:
                load(which, h).start()

    barrier = pltpu.get_barrier_semaphore()

    @pl.when(me > 0)
    def _():
        pl.semaphore_signal(barrier, inc=1, device_id={"seq": lax.rem(me + n_seq - 1, n_seq)}, device_id_type=MESH)

    for d in range(1, n_head):
        pl.semaphore_signal(barrier, inc=1, device_id={"head": lax.rem(mh + d, n_head)}, device_id_type=MESH)

    loads_of((0, 1))

    upper = jnp.where(
        lax.broadcasted_iota(jnp.int32, (rows, rows), 0) <= lax.broadcasted_iota(jnp.int32, (rows, rows), 1), 1.0, 0.0
    ).astype(BF16)
    rest = dec_ref[...]
    sums = jnp.zeros_like(rest)
    for _ in range(3):
        piece = rest.astype(BF16)
        rest = rest - piece.astype(F32)
        sums = sums + mm(piece, upper, 1, 0)
    crow[...] = sums * LOG2E

    def prepare():
        loads_of((2, 3))
        down = lax.broadcasted_iota(jnp.int32, (half, half), 0)
        across = lax.broadcasted_iota(jnp.int32, (half, half), 1)
        mask[...] = jnp.where(down >= across, 0.0, -1e30)
        mask_t[...] = jnp.where(down <= across, 0.0, -1e30)
        acc_a[...] = jnp.zeros_like(acc_a)
        acc_p[...] = jnp.zeros_like(acc_p)

        @pl.when(me == 0)
        def _():
            recv_f[...] = jnp.zeros_like(recv_f)

        @pl.when(me == n_seq - 1)
        def _():
            recv_b[...] = jnp.zeros_like(recv_b)

    strip = D // CUT

    def forth(h, c):
        here = pl.ds(c * strip, strip)
        return pltpu.make_async_remote_copy(
            src_ref=send_f.at[h, here, :], dst_ref=recv_f.at[h, here, :],
            send_sem=fs_sem.at[h, c], recv_sem=fr_sem.at[h, c],
            device_id={"seq": lax.rem(me + 1, n_seq)}, device_id_type=MESH)

    def back(h, c):
        here = pl.ds(c * strip, strip)
        return pltpu.make_async_remote_copy(
            src_ref=send_b.at[h, here, :], dst_ref=recv_b.at[h, here, :],
            send_sem=bs_sem.at[h, c], recv_sem=br_sem.at[h, c],
            device_id={"seq": lax.rem(me + n_seq - 1, n_seq)}, device_id_type=MESH)

    def link(h, c, copy, sent, received, first, last):
        @pl.when(jnp.logical_not(first))
        def _():
            here = pl.ds(c * strip, strip)
            decay = jnp.exp2(ccol[h, rows - 1:rows, :])
            copy(h, c).wait_recv()

            @pl.when(jnp.logical_not(last))
            def _():
                sent[h, here, :] = decay * received[h, here, :] + sent[h, here, :]
                copy(h, c).start()

    def rising(h):
        return jnp.exp2(ccol[h])

    def falling(h):
        c = ccol[h]
        return jnp.exp2(c[rows - 1:rows] - c)

    def scaled(x, factor):
        return (x.astype(F32) * factor).astype(BF16)

    def own_states(i):
        some = [i * group + u for u in range(group)]
        for h in some:
            load(0, h).wait()
            load(1, h).wait()
        cols = [jnp.broadcast_to(crow[pl.ds(h, 1), :], (D, rows)).T for h in some]
        falls = [jnp.exp2(c[rows - 1:rows] - c) for c in cols]
        states = [mm(scaled(k[h], f), v[h], 0, 0) for h, f in zip(some, falls)]
        for h, c, state in zip(some, cols, states):
            ccol[h] = c
            send_f[h] = state

    groups = heads // group
    source_f = (me == 0) & (n_seq > 1)
    source_b = (me == n_seq - 1) & (n_seq > 1)

    def send(i, copy):
        for u in range(group):
            for c in range(CUT):
                copy(i * group + u, c).start()

    def send_soon(i, copy, source):
        @pl.when(source & ((i == 0) | jnp.logical_not(odd)))
        def _():
            send(i, copy)

    own_states(0)
    pl.semaphore_wait(barrier, n_head - 1 + jnp.where(me < n_seq - 1, 1, 0))
    send_soon(0, forth, source_f)
    prepare()

    lead = jnp.where(me == 1, min(LEAD, groups), groups)

    @pl.loop(1, lead)
    def _(i):
        own_states(i)
        send_soon(i, forth, source_f)

    def wide(h, lo, hi, width):
        c = ccol[h, lo:hi, :]
        return jnp.concatenate([c] * (width // D), axis=1)

    def weigh(h, t, s, raw):
        spread = wide(h, t, t + half, half) - crow[pl.ds(h, 1), s:s + half]
        if s == t:
            spread = spread + mask[...]
        return (raw * jnp.exp2(spread)).astype(BF16)

    def weigh_t(h, s, t, raw):
        spread = crow[pl.ds(h, 1), t:t + half] - wide(h, s, s + half, half)
        if s == t:
            spread = spread + mask_t[...]
        return (raw * jnp.exp2(spread)).astype(BF16)

    def lower(h, a, b):
        a0, a1, b0, b1 = a[0:half], a[half:rows], b[0:half], b[half:rows]
        return (
            weigh(h, 0, 0, mm(a0, b0, 1, 1)),
            weigh(h, half, 0, mm(a1, b0, 1, 1)),
            weigh(h, half, half, mm(a1, b1, 1, 1)),
        )

    def upper_t(h, a, b):
        a0, a1, b0, b1 = a[0:half], a[half:rows], b[0:half], b[half:rows]
        return (
            weigh_t(h, 0, 0, mm(a0, b0, 1, 1)),
            weigh_t(h, 0, half, mm(a0, b1, 1, 1)),
            weigh_t(h, half, half, mm(a1, b1, 1, 1)),
        )

    def below(tiles, x):
        return mm(tiles[0], x[0:half], 1, 0), mm(tiles[1], x[0:half], 1, 0) + mm(tiles[2], x[half:rows], 1, 0)

    def above(tiles, x):
        return mm(tiles[0], x[0:half], 1, 0) + mm(tiles[1], x[half:rows], 1, 0), mm(tiles[2], x[half:rows], 1, 0)

    def inner(h):
        x, y = q[h], k[h]
        qr[h] = scaled(x, rising(h))
        part[h, 0:half, :], part[h, half:rows, :] = below(lower(h, x, y), v[h])
        for n, tile in enumerate(upper_t(h, y, x)):
            st[h, n] = tile

    def outer(h):
        low = recv_f[h].astype(BF16)
        a = (part[h] + mm(qr[h], low, 1, 0)).astype(BF16)
        att[h] = a
        a = a.astype(F32)
        acc_a[...] += a * a
        acc_p[...] += og[h].astype(F32) * gain_ref[pl.ds(h, 1), :] * a

    def phase(pre, first, lag, more, ready, inside, join, after, turn):
        def start(i):
            @pl.when(i >= first)
            def _():
                more(i)

            ready(i)

        def begin(lo, hi):
            @pl.loop(lo, hi)
            def _(i):
                start(i)
                inside(i)
                turn(i)

        def joined(h, some):
            @pl.when(h >= first)
            def _():
                for c in some:
                    join(h, c)

        begin(0, pre)

        @pl.loop(0, first)
        def _(h):
            more(h)
            for c in range(CUT):
                join(h, c)

        begin(pre, lag)

        @pl.loop(lag, heads)
        def _(i):
            start(i)
            joined(i - lag, (0,))
            inside(i)
            joined(i - lag, range(1, CUT))
            after(i - lag)

        @pl.loop(heads - lag, heads)
        def _(i):
            joined(i, range(CUT))
            after(i)

    def ready_f(h):
        load(2, h).wait()
        load(3, h).wait()

    def more_f(h):
        at = h // group + lead

        @pl.when((h % group == 0) & (at < groups))
        def _():
            own_states(at)

    def join_f(h, c):
        link(h, c, forth, send_f, recv_f, me == 0, me == n_seq - 1)

    def join_b(h, c):
        if c == 0:
            @pl.when((me == 0) & (h == heads - 1))
            def _():
                gather_gain()

        link(h, c, back, send_b, recv_b, me == n_seq - 1, me == 0)
        if c == 0:
            @pl.when(h == 0)
            def _():
                for d in range(1, n_seq):
                    share_gain(d, me).start()

    def held(copy, source, at):
        def turn(i):
            @pl.when(source & odd & (i == at))
            def _():
                @pl.loop(1, groups)
                def _(j):
                    send(j, copy)
        return turn

    def plan(done, left, each):
        relay = (done > 0) & (left > 0)
        wait = jnp.clip(each * (done - 1), 0, heads)
        first = jnp.where(relay, jnp.where(odd, group, heads), 0)
        lag = jnp.where(odd, heads, wait)
        return jnp.where(relay, wait, lag), first, lag

    phase(*plan(me, n_seq - 1 - me, LAG_F), more_f, ready_f, inner, join_f, outer, held(forth, source_f, min(HOLD_F, heads - 1)))

    stat[mh, 0:1, :] = jnp.sum(acc_a[...].T, axis=0, keepdims=True)
    stat[mh, 1:2, :] = jnp.sum(acc_p[...].T, axis=0, keepdims=True)

    def share_stat(d, slot):
        return pltpu.make_async_remote_copy(
            src_ref=stat.at[mh], dst_ref=stat.at[slot], send_sem=ss_sem.at[d], recv_sem=sr_sem.at[slot],
            device_id={"head": lax.rem(mh + d, n_head)}, device_id_type=MESH)

    for d in range(1, n_head):
        share_stat(d, mh).start()
    for d in range(1, n_head):
        share_stat(d, lax.rem(mh + d, n_head)).wait_recv()
    sums = stat[0]
    for j in range(1, n_head):
        sums = sums + stat[j]
    scale = lax.rsqrt(sums[0:1] / features + EPS)
    inv[...] = jnp.broadcast_to(scale, (D, rows)).T
    prj[...] = jnp.broadcast_to(scale * (sums[1:2] / features), (D, rows)).T

    @pl.loop(0, heads // group)
    def _(i):
        some = [i * group + u for u in range(group)]
        grads, states = [], []
        for h in some:
            g = gain_ref[pl.ds(h, 1), :]
            o = og[h].astype(F32)
            r = inv[...]
            normed = att[h].astype(F32) * r
            grad = (r * (o * g - normed * prj[...])).astype(BF16)
            states.append(mm(qr[h], grad, 0, 0))
            grads.append((grad, (normed * g).astype(BF16), jnp.sum(o * normed, axis=0, keepdims=True)))
        for h, (grad, out, gain), state in zip(some, grads, states):
            send_b[h] = state
            ga[h] = grad
            no[:, lanes(h)] = out
            ggs[me, pl.ds(h, 1), :] = gain

        @pl.when(source_b)
        def _():
            send(i, back)

    def share_gain(d, slot):
        return pltpu.make_async_remote_copy(
            src_ref=ggs.at[me], dst_ref=ggs.at[slot], send_sem=gs_sem.at[d], recv_sem=gr_sem.at[slot],
            device_id={"seq": lax.rem(me + d, n_seq)}, device_id_type=MESH)

    def gather_gain():
        for d in range(1, n_seq):
            share_gain(d, lax.rem(me + d, n_seq)).wait_recv()
        total = ggs[0]
        for j in range(1, n_seq):
            total = total + ggs[j]
        gg_ref[...] = total
        for d in range(1, n_seq):
            share_gain(d, me).wait_send()

    @pl.when(me < n_seq - 1)
    def _():
        @pl.loop(0, heads)
        def _(h):
            for c in range(CUT):
                forth(h, c).wait_send()

    for d in range(1, n_head):
        share_stat(d, mh).wait_send()

    def inner_back(h):
        grad, x, y, z = ga[h], q[h], k[h], v[h]
        top, bottom = below(lower(h, grad, z), y)
        up = mm(scaled(grad, rising(h)), recv_f[h].astype(BF16), 1, 1)
        part[h, 0:half, :], part[h, half:rows, :] = above(upper_t(h, z, grad), x)
        part2[h, 0:half, :], part2[h, half:rows, :] = above([st[h, n] for n in range(3)], grad)
        gq[0:half, lanes(h)] = (top + up[0:half]).astype(BF16)
        gq[half:rows, lanes(h)] = (bottom + up[half:rows]).astype(BF16)
        fall = falling(h)
        k[h] = scaled(y, fall)
        v[h] = scaled(z, fall)

    def outer_back(h):
        low = recv_b[h].astype(BF16)
        gk[:, lanes(h)] = (part[h] + mm(v[h], low, 1, 1)).astype(BF16)
        gv[:, lanes(h)] = (part2[h] + mm(k[h], low, 1, 0)).astype(BF16)

    behind = jnp.clip(LAG_B * (n_seq - 2 - me), 0, heads)
    phase(behind, 0, behind, lambda h: None, lambda h: None, inner_back, join_b, outer_back, lambda i: None)

    @pl.when(me > 0)
    def _():
        gather_gain()

        @pl.loop(0, heads)
        def _(h):
            for c in range(CUT):
                back(h, c).wait_send()


def store(heads, *refs):
    sources, targets, sem = refs[:5], refs[5:10], refs[10]
    copies = []
    for n, (source, target) in enumerate(zip(sources, targets)):
        parts = PIECES if n < 4 else 1
        size = source.shape[0] // parts
        for p in range(parts):
            here = pl.ds(p * size, size)
            copies.append(pltpu.make_async_copy(source.at[here, :], target.at[here, :], sem.at[n, p]))
    for copy in copies:
        copy.start()
    for copy in copies:
        copy.wait()


def local(n_seq, n_head, queries, key_vectors, values, decay_log, norm_gain, out_grad):
    rows, width = queries.shape
    heads = decay_log.shape[0]
    big = pltpu.VMEM((rows, width), BF16)
    hbm = pl.BlockSpec(memory_space=pl.ANY)
    vmem = pl.BlockSpec(memory_space=pltpu.VMEM)
    low = pltpu.VMEM((heads, rows, D), BF16)
    full = pltpu.VMEM((heads, rows, D), F32)
    state = pltpu.VMEM((heads, D, D), F32)
    plane = pltpu.VMEM((rows, D), F32)
    tile = pltpu.VMEM((rows // 2, rows // 2), F32)
    gain = jax.ShapeDtypeStruct((heads, D), F32)
    small = pltpu.VMEM((heads, D), F32)
    dma = pltpu.SemaphoreType.DMA
    outs = pl.pallas_call(
        functools.partial(kernel, n_seq, n_head, heads, rows, width * n_head),
        out_shape=(big, big, big, big, small),
        in_specs=[hbm, hbm, hbm, vmem, vmem, hbm],
        out_specs=(vmem, vmem, vmem, vmem, vmem),
        scratch_shapes=[
            low, low, low, low, low, low, pltpu.VMEM((heads, 3, rows // 2, rows // 2), BF16), full,
            pltpu.VMEM((heads, rows), F32), tile, tile, full, full,
            low, state, state, state, state, plane, plane, plane, plane,
            pltpu.VMEM((n_head, 2, rows), F32), pltpu.VMEM((n_seq, heads, D), F32),
            dma((4, heads)), dma((heads, CUT)), dma((heads, CUT)), dma((heads, CUT)), dma((heads, CUT)),
            dma((n_head,)), dma((n_head,)), dma((n_seq,)), dma((n_seq,)),
        ],
        compiler_params=pltpu.CompilerParams(
            collective_id=0, has_side_effects=True, vmem_limit_bytes=50 * 2**20),
    )(queries, key_vectors, values, decay_log, norm_gain.reshape(heads, D), out_grad)
    wide = jax.ShapeDtypeStruct((rows, width), BF16)
    outs = pl.pallas_call(
        functools.partial(store, heads),
        out_shape=(wide, wide, wide, wide, gain),
        in_specs=[vmem] * 5,
        out_specs=(hbm,) * 5,
        scratch_shapes=[dma((5, PIECES))],
        compiler_params=pltpu.CompilerParams(vmem_limit_bytes=2**20),
    )(*[pltpu.with_memory_space_constraint(out, pltpu.VMEM) for out in outs])
    return outs[:4] + (outs[4].reshape(heads * D),)


def solution(mesh):
    wide = P(("grp", "seq"), "head")
    return jax.shard_map(
        functools.partial(local, mesh.shape["seq"], mesh.shape["head"]),
        mesh=mesh,
        in_specs=(wide, wide, wide, P("head", ("grp", "seq")), P("head"), wide),
        out_specs=(wide, wide, wide, wide, P(("grp", "head"))),
        check_vma=False,
    )
```
